32 devices in a mesh: dp: 8 (over y, x, core), ctx: 4 (over z).
Axes of the slice: x: 2, y: 2, z: 4, core: 2. Of those that a mesh axis runs over, the one named last changes fastest.
Arguments:
- layer_input: bfloat16 [8, 1024, 2048], P('dp', 'ctx'), may hold values from -6 to 6
- block_ids: int32 [8, 1024], P('dp'), may hold values from 0 to 7, never falling along the last dimension, each value on 1 to 256 neighbouring positions
- out_grad: bfloat16 [8, 1024, 2048], P('dp', 'ctx'), may hold values from -6 to 6
- qkv_weight: bfloat16 [2048, 3, 2048], P('dp', None, 'ctx'), may hold values from -0.125 to 0.125
- out_weight: bfloat16 [2048, 2048], P('ctx', 'dp'), may hold values from -1 to 1
- up_weight: bfloat16 [2048, 8192], P('dp', 'ctx'), may hold values from -0.125 to 0.125
- down_weight: bfloat16 [8192, 2048], P('ctx', 'dp'), may hold values from -0.0625 to 0.0625
- attn_gain: bfloat16 [2048], P(('dp', 'ctx')), may hold values from 0.25 to 1.75
- attn_shift: bfloat16 [2048], P(('dp', 'ctx')), may hold values from -1 to 1
- query_bias: bfloat16 [2048], P(('dp', 'ctx')), may hold values from -0.5 to 0.5
- value_bias: bfloat16 [2048], P(('dp', 'ctx')), may hold values from -0.14941406 to 0.14941406
- out_bias: bfloat16 [2048], P(('dp', 'ctx')), may hold values from -0.5 to 0.5
- mlp_gain: bfloat16 [2048], P(('dp', 'ctx')), may hold values from 0.25 to 1.75
- mlp_shift: bfloat16 [2048], P(('dp', 'ctx')), may hold values from -1 to 1
- up_bias: bfloat16 [8192], P(('dp', 'ctx')), may hold values from -0.5 to 0.5
- down_bias: bfloat16 [2048], P(('dp', 'ctx')), may hold values from -0.5 to 0.5
Outputs:
- layer_output: bfloat16 [8, 1024, 2048], P('dp', 'ctx')
- input_grad: float32 [8, 1024, 2048], P('dp', 'ctx')
- grad_qkv_weight: float32 [2048, 3, 2048], P('dp', None, 'ctx')
- grad_out_weight: float32 [2048, 2048], P('ctx', 'dp')
- grad_up_weight: float32 [2048, 8192], P('dp', 'ctx')
- grad_down_weight: float32 [8192, 2048], P('ctx', 'dp')
- grad_attn_gain: float32 [2048], P(('dp', 'ctx'))
- grad_attn_shift: float32 [2048], P(('dp', 'ctx'))
- grad_query_bias: float32 [2048], P(('dp', 'ctx'))
- grad_value_bias: float32 [2048], P(('dp', 'ctx'))
- grad_out_bias: float32 [2048], P(('dp', 'ctx'))
- grad_mlp_gain: float32 [2048], P(('dp', 'ctx'))
- grad_mlp_shift: float32 [2048], P(('dp', 'ctx'))
- grad_up_bias: float32 [8192], P(('dp', 'ctx'))
- grad_down_bias: float32 [2048], P(('dp', 'ctx'))
The draws below stay inside these ranges and needn't reach their ends.
Inputs may be any that keep to these rules, and one draw needn't show every extreme that they name: `block_ids`: block numbers never fall along a sequence; every number from 0 to the largest is used; a block holds 1 to 256 tokens of one sequence, and some block holds exactly 256.
All inputs are finite; a program needn't handle non-finite values.
Results may differ from the reference program's by a relative error of at most 0.018.
Values may be sent and summed in bfloat16 or wider, within the bound.
No kernel may reach another device: no remote copies, remote signals or barrier semaphores. Data moves between devices by JAX's collectives and lax.ppermute only.
A program may use at most 448 MiB of HBM per device.

```python
import math
import jax
import jax.numpy as jnp
import numpy as np
from jax import lax

D = 2048
HEADS = 16
HEAD_DIM = 128
FF = 8192
SEQS = 1
SEQ_LEN = 1024
BLOCK = 256
NSEQ = 8
N_DP = 8


def shard_levels(own_key, shape, cuts, least, top_value):
    loudness = 1.0
    for position, parts in cuts:
        heights = jax.random.uniform(jax.random.fold_in(jax.random.fold_in(own_key, 6), position), (parts,), jnp.float32, least / len(cuts), top_value / len(cuts))
        loudness = loudness * jnp.repeat(jnp.exp(heights), shape[position] // parts).reshape((-1,) + (1,) * (len(shape) - 1 - position))
    return loudness


def profile(amount, total, most, skew):
    portions = [(1 << 20) // math.isqrt(grade ** skew) + 1 for grade in range(2, amount + 1)]
    rest, counts = total - most - (amount - 1), [1] * (amount - 1)
    while rest > 0:
        movable = [i for i in range(amount - 1) if counts[i] < most]
        mass, left = sum([portions[i] for i in movable]), rest
        for i in movable:
            more = min(most - counts[i], max(1, left * portions[i] // mass), rest)
            counts[i] = counts[i] + more
            rest = rest - more
    return np.array([most] + counts)


def uneven_parts(rng, number_of, total, most, skew):
    if number_of == 2:
        one = jax.random.randint(rng, (), max(1, total - most), min(most, total - 1) + 1)
        return jnp.stack([one, total - one])
    lengths = jnp.asarray(profile(number_of, total, most, skew), jnp.int32)
    pairs = (number_of - 1) // 2
    donor, taker = lengths[1:1 + 2 * pairs:2], lengths[2:2 + 2 * pairs:2]
    margin = jnp.minimum(donor - 1, most - taker)
    shifted = jax.random.randint(jax.random.fold_in(rng, 1), (pairs,), 0, 1 << 20) % (margin + 1)
    lengths = lengths.at[1:1 + 2 * pairs:2].set(donor - shifted).at[2:2 + 2 * pairs:2].set(taker + shifted)
    return lengths[jax.random.permutation(jax.random.fold_in(rng, 2), number_of)]


def normal_values(stream_key, extent, width, reach, cuts=(), held_as=jnp.bfloat16):
    values = jax.random.normal(stream_key, extent, jnp.float32) * width
    if len(cuts) > 0:
        values = shard_levels(stream_key, extent, cuts, -0.22, 0.18) * values
    return jnp.clip(values, min=-reach, max=reach).astype(held_as)


def setup_inputs(seed: int = 0) -> dict:
    seeds = jax.random.split(jax.random.key(seed), 17)
    return {
        "layer_input": normal_values(seeds[0], (NSEQ, SEQ_LEN, D), 1.0, 6.0, ((0, 8), (1, 4))),
        "block_ids": jax.vmap(lambda own: jnp.searchsorted(jnp.cumsum(uneven_parts(own, 2 * SEQ_LEN // BLOCK, SEQ_LEN, BLOCK, 1)), jnp.arange(SEQ_LEN), side="right"))(jax.random.split(seeds[1], NSEQ)).reshape((NSEQ, SEQ_LEN)).astype(jnp.int32),
        "out_grad": normal_values(seeds[2], (NSEQ, SEQ_LEN, D), 1.0, 6.0, ((0, 8), (1, 4))),
        "qkv_weight": normal_values(seeds[3], (D, 3, D), D ** -0.5, 0.125, ((0, 8), (2, 4))),
        "out_weight": normal_values(seeds[4], (D, D), (D // 64) ** -0.5, 1.0, ((0, 4), (1, 8))),
        "up_weight": normal_values(seeds[5], (D, FF), D ** -0.5, 0.125, ((0, 8), (1, 4))),
        "down_weight": normal_values(seeds[6], (FF, D), FF ** -0.5, 0.0625, ((0, 4), (1, 8))),
        "attn_gain": jnp.clip(1.0 + 0.15 * jax.random.normal(seeds[7], (D,), jnp.float32), 0.25, 1.75).astype(jnp.bfloat16),
        "attn_shift": normal_values(seeds[8], (D,), 0.2, 1.0, ((0, 32),)),
        "query_bias": normal_values(seeds[9], (D,), 0.1, 0.5, ((0, 32),)),
        "value_bias": normal_values(seeds[10], (D,), 0.03, 0.14941406, ((0, 32),)),
        "out_bias": normal_values(seeds[11], (D,), 0.1, 0.5, ((0, 32),)),
        "mlp_gain": jnp.clip(1.0 + 0.15 * jax.random.normal(seeds[12], (D,), jnp.float32), 0.25, 1.75).astype(jnp.bfloat16),
        "mlp_shift": normal_values(seeds[13], (D,), 0.2, 1.0, ((0, 32),)),
        "up_bias": normal_values(seeds[14], (FF,), 0.1, 0.5, ((0, 32),)),
        "down_bias": normal_values(seeds[15], (D,), 0.1, 0.5, ((0, 32),)),
    }


@jax.custom_vjp
def low(v):
    return lax.optimization_barrier(v.astype(jnp.bfloat16)).astype(jnp.float32)

@jax.custom_vjp
def low_back(v):
    return v

def low_keep(v):
    return (low(v), None)

def low_pass(kept, grad):
    return (grad,)

def back_keep(v):
    return (v, None)

def back_low(kept, grad):
    return (low(grad),)
low.defvjp(low_keep, low_pass)
low_back.defvjp(back_keep, back_low)
EXACT = lax.Precision.HIGHEST

def product(left, right):
    return jnp.dot(left, right, preferred_element_type=jnp.float32, precision=EXACT)

def layer_norm(values, gain, shift):
    middle = lax.optimization_barrier(jnp.mean(values, axis=-1, keepdims=True))
    centred = values - middle
    spread = lax.optimization_barrier(jnp.mean(centred * centred, axis=-1, keepdims=True))
    return centred * lax.rsqrt(spread + 1e-05) * gain + shift

def attend_block(queries, keys_all, values_all, query_ids, key_ids):
    scores = jnp.einsum('qhd,khd->hqk', queries, keys_all, precision=EXACT) * (1.0 / math.sqrt(HEAD_DIM))
    scores = low_back(scores)
    visible = key_ids[None, None, :] <= query_ids[None, :, None]
    masked = jnp.where(visible, scores, -1e+30)
    highest = lax.optimization_barrier(jnp.max(masked, axis=-1, keepdims=True))
    log_total = highest + jnp.log(lax.optimization_barrier(jnp.sum(jnp.exp(masked - highest), axis=-1, keepdims=True)))
    weights = low(jnp.exp(masked - log_total))
    return jnp.einsum('hqk,khd->qhd', weights, values_all, precision=EXACT)

def attend_sequence(operands):
    queries, keys_all, values_all, seq_ids = operands
    block_rows = min(512, SEQ_LEN)
    pieces = []
    for offset in range(0, SEQ_LEN, block_rows):
        pieces.append(jax.checkpoint(attend_block)(queries[offset:offset + block_rows], keys_all, values_all, seq_ids[offset:offset + block_rows], seq_ids))
    return jnp.concatenate(pieces, axis=0)

def forward(group_x, group_ids, params):
    qkv_w, out_w, up_w, down_w, gain_one, shift_one, bias_query, bias_value, bias_out, gain_two, shift_two, bias_up, bias_down = params
    qkv_w = qkv_w.reshape(D, 3 * D)
    group_seqs = group_x.shape[0]
    flat_rows = group_x.reshape(group_seqs * SEQ_LEN, D)
    act_one = low(layer_norm(flat_rows, gain_one, shift_one))
    joined = product(act_one, qkv_w)
    queries = low_back(low(joined[:, :D] + bias_query))
    keys_all = low_back(low(joined[:, D:2 * D]))
    values_all = low_back(low(joined[:, 2 * D:] + bias_value))
    head_shape = (group_seqs, SEQ_LEN, HEADS, HEAD_DIM)
    attended = lax.map(attend_sequence, (queries.reshape(head_shape), keys_all.reshape(head_shape), values_all.reshape(head_shape), group_ids))
    attended = low_back(low(attended.reshape(group_seqs * SEQ_LEN, D)))
    after_attn = flat_rows + low_back(product(attended, out_w) + bias_out)
    act_two = low(layer_norm(after_attn, gain_two, shift_two))
    pre_act = low_back(product(act_two, up_w) + bias_up)
    hidden = low(jax.nn.gelu(pre_act, approximate=False))
    result = after_attn + product(hidden, down_w) + bias_down
    return result.reshape(group_x.shape)

def reference(layer_input, block_ids, out_grad, qkv_weight, out_weight, up_weight, down_weight, attn_gain, attn_shift, query_bias, value_bias, out_bias, mlp_gain, mlp_shift, up_bias, down_bias):
    params = tuple((tensor.astype(jnp.float32) for tensor in (qkv_weight, out_weight, up_weight, down_weight, attn_gain, attn_shift, query_bias, value_bias, out_bias, mlp_gain, mlp_shift, up_bias, down_bias)))
    grouped_x = layer_input.astype(jnp.float32).reshape(N_DP, SEQS, SEQ_LEN, D)
    grouped_ids = block_ids.reshape(N_DP, SEQS, SEQ_LEN)
    grouped_grad = out_grad.astype(jnp.float32).reshape(N_DP, SEQS, SEQ_LEN, D)

    def one_group(totals, operands):
        group_x, group_ids, group_grad = operands
        result, pullback = jax.vjp(lambda inner_x, inner_p: forward(inner_x, group_ids, inner_p), group_x, params)
        grad_x, grad_p = pullback(group_grad)
        totals = jax.tree.map(lambda left, right: left + right, totals, grad_p)
        return (totals, (result.astype(jnp.bfloat16), grad_x))
    start_totals = tuple((jnp.zeros_like(tensor) for tensor in params))
    totals, (outputs, grads) = lax.scan(one_group, start_totals, (grouped_x, grouped_ids, grouped_grad))
    return (outputs.reshape(NSEQ, SEQ_LEN, D), grads.reshape(NSEQ, SEQ_LEN, D), totals[0], totals[1], totals[2], totals[3], totals[4], totals[5], totals[6], totals[7], totals[8], totals[9], totals[10], totals[11], totals[12])
```

```python
import functools
import math

import jax
import jax.numpy as jnp
from jax import lax
from jax.experimental import pallas as pl
from jax.experimental.pallas import tpu as pltpu
from jax.sharding import PartitionSpec as P

HEAD_DIM = 128
SCALE = 1.0 / math.sqrt(HEAD_DIM)
BF16 = jnp.bfloat16
F32 = jnp.float32
LAST = (((1,), (1,)), ((), ()))
FIRST = (((0,), (0,)), ((), ()))


def mm(left, right):
    return jnp.dot(left, right, preferred_element_type=F32)


def mm_nt(left, right):
    return lax.dot_general(left, right, LAST, preferred_element_type=F32)


def mm_tn(left, right):
    return lax.dot_general(left, right, FIRST, preferred_element_type=F32)


def normalize(values, gain, shift):
    middle = jnp.mean(values, axis=-1, keepdims=True)
    centred = values - middle
    spread = jnp.mean(centred * centred, axis=-1, keepdims=True)
    inv_std = lax.rsqrt(spread + 1e-05)
    unit_rows = centred * inv_std
    return (unit_rows * gain + shift, unit_rows, inv_std)


def normalize_back(grad_rows, gain, unit_rows, inv_std):
    scaled = grad_rows * gain
    centred = scaled - jnp.mean(scaled, axis=-1, keepdims=True)
    centred = centred - unit_rows * jnp.mean(scaled * unit_rows, axis=-1, keepdims=True)
    return (centred * inv_std, jnp.sum(grad_rows * unit_rows, axis=0), jnp.sum(grad_rows, axis=0))


def forward_kernel(q_ref, k_ref, v_ref, col_ref, row_ref, o_ref, lt_ref):
    slots, _, span, _ = q_ref.shape
    keys = k_ref[...].reshape(slots * span, HEAD_DIM)
    values_t = v_ref[...].reshape(slots * span, HEAD_DIM).T
    key_ids = col_ref[0]
    for slot in range(slots):
        scores = mm_nt(keys, q_ref[slot, 0]) * SCALE
        query_ids = row_ref[0, :, slot * span : (slot + 1) * span]
        scores = jnp.where(key_ids <= query_ids, scores, -1e30)
        highest = jnp.max(scores, axis=0, keepdims=True)
        weights = jnp.exp(scores - highest)
        total = jnp.sum(weights, axis=0, keepdims=True)
        probs = (weights * (1.0 / total)).astype(BF16)
        o_ref[slot, 0] = mm(values_t, probs).T.astype(BF16)
        lt_ref[0, 0, :, slot * span : (slot + 1) * span] = highest + jnp.log(total)


def backward_kernel(
    q_ref, k_ref, v_ref, o_ref, do_ref, col_ref, row_ref, lt_ref, dq_ref, dk_ref, dv_ref, ka_ref, va_ref
):
    slots, _, span, _ = q_ref.shape
    keys = k_ref[...].reshape(slots * span, HEAD_DIM)
    keys_t = keys.T
    values = v_ref[...].reshape(slots * span, HEAD_DIM)
    key_ids = col_ref[0]
    for slot in range(slots):
        queries = q_ref[slot, 0]
        grad_out = do_ref[slot, 0]
        scores = mm_nt(keys, queries) * SCALE
        query_ids = row_ref[0, :, slot * span : (slot + 1) * span]
        log_total = lt_ref[0, 0, :, slot * span : (slot + 1) * span]
        probs = jnp.exp(jnp.where(key_ids <= query_ids, scores, -1e30) - log_total)
        inner = grad_out.astype(F32) * o_ref[slot, 0].astype(F32)
        inner = jnp.sum(inner.T, axis=0, keepdims=True)
        grad_scores = (probs * (mm_nt(values, grad_out) - inner)).astype(BF16)
        dq_ref[slot, 0] = (mm(keys_t, grad_scores) * SCALE).T.astype(BF16)
        key_part = mm(grad_scores, queries)
        value_part = mm(probs.astype(BF16), grad_out)
        if slot == 0:
            ka_ref[...] = key_part
            va_ref[...] = value_part
        else:
            ka_ref[...] += key_part
            va_ref[...] += value_part
    dk_ref[...] = (ka_ref[...] * SCALE).astype(BF16).reshape(dk_ref.shape)
    dv_ref[...] = va_ref[...].astype(BF16).reshape(dv_ref.shape)


def head_specs(slots, span, heads):
    def at(offset):
        return pl.BlockSpec((slots, 1, span, HEAD_DIM), lambda s, h: (0, s, 0, offset + h))

    col = pl.BlockSpec((1, slots * span, 1), lambda s, h: (s, 0, 0))
    row = pl.BlockSpec((1, 1, slots * span), lambda s, h: (s, 0, 0))
    total = pl.BlockSpec((1, 1, 1, slots * span), lambda s, h: (s, h, 0, 0))
    return (at(0), at(heads), at(2 * heads), col, row, total)


def attend_forward(joined, ids_col, ids_row):
    slots, seqs, span, width = joined.shape
    heads = width // (3 * HEAD_DIM)
    q, k, v, col, row, total = head_specs(slots, span, heads)
    return pl.pallas_call(
        forward_kernel,
        grid=(seqs, heads),
        in_specs=[q, k, v, col, row],
        out_specs=[q, total],
        out_shape=[
            jax.ShapeDtypeStruct((slots, seqs, span, heads * HEAD_DIM), BF16),
            jax.ShapeDtypeStruct((seqs, heads, 1, slots * span), F32),
        ],
        name="attend_forward",
    )(joined, joined, joined, ids_col, ids_row)


def attend_backward(joined, attended, grad_attended, ids_col, ids_row, log_total):
    slots, seqs, span, width = joined.shape
    heads = width // (3 * HEAD_DIM)
    q, k, v, col, row, total = head_specs(slots, span, heads)
    shape = jax.ShapeDtypeStruct((slots, seqs, span, heads * HEAD_DIM), BF16)
    return pl.pallas_call(
        backward_kernel,
        grid=(seqs, heads),
        in_specs=[q, k, v, q, q, col, row, total],
        out_specs=[q, q, q],
        out_shape=[shape, shape, shape],
        scratch_shapes=[pltpu.VMEM((slots * span, HEAD_DIM), F32)] * 2,
        name="attend_backward",
    )(joined, joined, joined, attended, grad_attended, ids_col, ids_row, log_total)


def after(value, *others):
    return lax.optimization_barrier((value,) + others)[0]


def shards(
    n,
    m,
    layer_input,
    block_ids,
    out_grad,
    qkv_weight,
    out_weight,
    up_weight,
    down_weight,
    attn_gain,
    attn_shift,
    query_bias,
    value_bias,
    out_bias,
    mlp_gain,
    mlp_shift,
    up_bias,
    down_bias,
):
    seqs, span, width = layer_input.shape
    rows = seqs * span
    pos = lax.axis_index("ctx")
    cols = qkv_weight.shape[2]
    hidden_cols = up_weight.shape[1]

    def move(value, shift):
        return lax.ppermute(value, "ctx", [(i, (i + shift) % n) for i in range(n)])

    def ring_gather(value, shift=1):
        slots = [value]
        for _ in range(n - 1):
            slots.append(move(slots[-1], shift))
        return slots

    def ring_scatter(slots, shift=1):
        total = slots[1]
        for s in list(range(2, n)) + [0]:
            total = move(total.astype(BF16), shift).astype(F32) + slots[s].astype(F32)
        return total

    pieces = (
        attn_gain,
        attn_shift,
        query_bias,
        value_bias,
        out_bias,
        mlp_gain,
        mlp_shift,
        down_bias,
        up_bias,
    )
    packed = jnp.concatenate(pieces)
    packed_size = packed.shape[0]
    everyone = lax.all_to_all(jnp.broadcast_to(packed, (n, packed_size)), "ctx", 0, 0, tiled=True)
    everyone = lax.all_to_all(
        jnp.broadcast_to(everyone.reshape(1, n * packed_size), (m, n * packed_size)), "dp", 0, 0, tiled=True
    )
    everyone = everyone.reshape(m * n, packed_size).astype(F32)
    full = []
    offset = 0
    for piece in pieces:
        size = piece.shape[0]
        full.append(everyone[:, offset : offset + size].reshape(1, m * n * size))
        offset += size
    gain_one, shift_one, bias_query, bias_value, bias_out, gain_two, shift_two, bias_down, bias_up = full
    bias_query = lax.dynamic_slice_in_dim(bias_query, pos * cols, cols, 1)
    bias_value = lax.dynamic_slice_in_dim(bias_value, pos * cols, cols, 1)
    bias_up = lax.dynamic_slice_in_dim(bias_up, pos * hidden_cols, hidden_cols, 1)
    joined_bias = jnp.concatenate([bias_query, jnp.zeros_like(bias_query), bias_value], axis=1)

    qkv_full = lax.all_gather(qkv_weight.reshape(qkv_weight.shape[0], 3 * cols), "dp", axis=0, tiled=True)
    x_slots = ring_gather(layer_input.reshape(rows, width))
    out_chunks = ring_gather(out_weight.T, -1)
    out_t = lax.all_gather(jnp.concatenate(out_chunks, axis=1), "dp", axis=0, tiled=True)
    up_full = lax.all_gather(up_weight, "dp", axis=0, tiled=True)
    down_t = lax.all_gather(down_weight.T, "dp", axis=0, tiled=True)
    grad_low = out_grad.reshape(rows, width)
    dy_all = jnp.concatenate(ring_gather(after(grad_low, x_slots[-1])), axis=0)

    order = (pos - jnp.arange(n)) % n
    ids = jnp.take(block_ids.reshape(seqs, n, span), order, axis=1).reshape(seqs, n * span)
    ids_col = ids[:, :, None]
    ids_row = ids[:, None, :]

    resid = x_slots[0].astype(F32)
    _, unit_one, inv_one = normalize(resid, gain_one, shift_one)
    act_one = jnp.concatenate(
        [normalize(s.astype(F32), gain_one, shift_one)[0].astype(BF16) for s in x_slots], axis=0
    )
    joined = (mm(act_one, qkv_full) + joined_bias).astype(BF16).reshape(n, seqs, span, 3 * cols)
    attended, log_total = attend_forward(joined, ids_col, ids_row)
    mine = [attended[0].reshape(rows, cols)] + [
        move(attended[s].reshape(rows, cols), -s) for s in range(1, n)
    ]
    attended_rows = jnp.concatenate(mine, axis=1)
    after_attn = resid + mm_nt(attended_rows, out_t) + bias_out
    normed_two, unit_two, inv_two = normalize(after_attn, gain_two, shift_two)

    act_two = jnp.concatenate(ring_gather(normed_two.astype(BF16)), axis=0)
    pre_act = mm(act_two, up_full) + bias_up
    phi = 0.5 * (1.0 + lax.erf(pre_act * (1.0 / math.sqrt(2.0))))
    hidden = (pre_act * phi).astype(BF16)
    slope = phi + pre_act * (jnp.exp(-0.5 * pre_act * pre_act) * (1.0 / math.sqrt(2.0 * math.pi)))
    grad_pre = (mm(dy_all, down_t) * slope).astype(BF16)
    grad_act_two = ring_scatter(list(mm_nt(grad_pre, up_full).astype(BF16).reshape(n, rows, width)))
    grad_down_t = mm_tn(dy_all, hidden).astype(BF16)
    grad_up = mm_tn(act_two, grad_pre).astype(BF16)
    down_part = lax.psum_scatter(grad_down_t, "dp", scatter_dimension=0, tiled=True).astype(F32).T
    up_part = lax.psum_scatter(grad_up, "dp", scatter_dimension=0, tiled=True).astype(F32)
    grad_up_bias = jnp.sum(grad_pre, axis=0, dtype=F32)
    branch_out = list(mm_nt(hidden, down_t).astype(BF16).reshape(n, rows, width))

    grad_from_two, grad_gain_two, grad_shift_two = normalize_back(grad_act_two, gain_two, unit_two, inv_two)
    grad_top = grad_low.astype(F32)
    grad_after = grad_top + grad_from_two
    grad_branch = grad_after.astype(BF16)
    grad_attended_rows = mm(grad_branch, out_t).astype(BF16)
    sent = [grad_attended_rows[:, s * cols : (s + 1) * cols] for s in range(n)]
    grad_attended = jnp.stack([sent[0]] + [move(sent[s], s) for s in range(1, n)]).reshape(attended.shape)
    dq, dk, dv = attend_backward(joined, attended, grad_attended, ids_col, ids_row, log_total)
    layer_output = after_attn + ring_scatter([after(b, grad_act_two) for b in branch_out]) + bias_down
    grad_joined = jnp.concatenate([dq, dk, dv], axis=3).reshape(n * rows, 3 * cols)
    grad_qkv = mm_tn(act_one, grad_joined).astype(BF16)
    qkv_part = lax.psum_scatter(grad_qkv, "dp", scatter_dimension=0, tiled=True).astype(F32)
    qkv_part = qkv_part.reshape(qkv_weight.shape)
    grad_act_one = ring_scatter(list(mm_nt(grad_joined, qkv_full).astype(BF16).reshape(n, rows, width)))
    grad_out_t = mm_tn(grad_branch, attended_rows).astype(BF16)
    out_part = lax.psum_scatter(grad_out_t, "dp", scatter_dimension=0, tiled=True)
    out_part = ring_scatter([out_part[:, s * cols : (s + 1) * cols] for s in range(n)], -1).T

    grad_from_one, grad_gain_one, grad_shift_one = normalize_back(grad_act_one, gain_one, unit_one, inv_one)
    input_grad = grad_after + grad_from_one
    grad_out_bias = jnp.sum(grad_branch, axis=0, dtype=F32)
    grad_down_bias = jnp.sum(grad_top, axis=0)
    sums = jnp.sum(grad_joined, axis=0, dtype=F32)

    def placed(part, length):
        return lax.dynamic_update_slice_in_dim(jnp.zeros((length,), F32), part, pos * part.shape[0], 0)

    vectors = (
        grad_gain_one,
        grad_shift_one,
        placed(sums[:cols], width),
        placed(sums[2 * cols :], width),
        grad_out_bias,
        grad_gain_two,
        grad_shift_two,
        grad_down_bias,
        placed(grad_up_bias, n * hidden_cols),
    )
    table = jnp.concatenate([v.reshape(m * n, -1) for v in vectors], axis=1)
    table = lax.all_to_all(table.reshape(m, n * packed_size), "dp", 0, 0, tiled=True)
    table = jnp.sum(table, axis=0).reshape(n, packed_size)
    table = jnp.sum(lax.all_to_all(table, "ctx", 0, 0, tiled=True), axis=0)
    vector_grads = []
    offset = 0
    for piece in pieces:
        size = piece.shape[0]
        vector_grads.append(table[offset : offset + size])
        offset += size
    g = vector_grads
    return (
        layer_output.astype(BF16).reshape(seqs, span, width),
        input_grad.reshape(seqs, span, width),
        qkv_part,
        out_part,
        up_part,
        down_part,
        g[0],
        g[1],
        g[2],
        g[3],
        g[4],
        g[5],
        g[6],
        g[8],
        g[7],
    )


def solution(mesh):
    vector = P(("dp", "ctx"))
    tokens = P("dp", "ctx", None)
    weights = (P("dp", None, "ctx"), P("ctx", "dp"), P("dp", "ctx"), P("ctx", "dp"))
    body = functools.partial(shards, mesh.shape["ctx"], mesh.shape["dp"])
    return jax.shard_map(
        body,
        mesh=mesh,
        in_specs=(tokens, P("dp", None), tokens) + weights + (vector,) * 9,
        out_specs=(tokens, tokens) + weights + (vector,) * 9,
        check_vma=False,
    )
```

```python
import functools
import math

import jax
import jax.numpy as jnp
from jax import lax
from jax.experimental import pallas as pl
from jax.experimental.pallas import tpu as pltpu
from jax.sharding import PartitionSpec as P


HEAD_DIM = 128
SCALE = 1.0 / math.sqrt(HEAD_DIM)
BF16 = jnp.bfloat16
F32 = jnp.float32
LAST = (((1,), (1,)), ((), ()))
FIRST = (((0,), (0,)), ((), ()))


def mm(left, right):
    return jnp.dot(left, right, preferred_element_type=F32)


def mm_nt(left, right):
    return lax.dot_general(left, right, LAST, preferred_element_type=F32)


def mm_tn(left, right):
    return lax.dot_general(left, right, FIRST, preferred_element_type=F32)


def normalize(values, gain, shift):
    middle = jnp.mean(values, axis=-1, keepdims=True)
    centred = values - middle
    spread = jnp.mean(centred * centred, axis=-1, keepdims=True)
    inv_std = lax.rsqrt(spread + 1e-05)
    unit_rows = centred * inv_std
    return (unit_rows * gain + shift, unit_rows, inv_std)


def normalize_back(grad_rows, gain, unit_rows, inv_std):
    scaled = grad_rows * gain
    centred = scaled - jnp.mean(scaled, axis=-1, keepdims=True)
    centred = centred - unit_rows * jnp.mean(scaled * unit_rows, axis=-1, keepdims=True)
    return (centred * inv_std, jnp.sum(grad_rows * unit_rows, axis=0), jnp.sum(grad_rows, axis=0))


def joined_slots(refs):
    return [ref.at[slot, 0] for ref in refs for slot in range(ref.shape[0])]


def forward_kernel(parts, *refs):
    q_slots = joined_slots(refs[:parts])
    k_slots = joined_slots(refs[parts : 2 * parts])
    v_slots = joined_slots(refs[2 * parts : 3 * parts])
    col_ref, row_ref, o_ref, lt_ref = refs[3 * parts :]
    span = q_slots[0].shape[0]
    keys = jnp.concatenate([r[...] for r in k_slots], axis=0)
    values_t = jnp.concatenate([r[...] for r in v_slots], axis=0).T
    key_ids = col_ref[0]
    for slot, q_ref in enumerate(q_slots):
        scores = mm_nt(keys, q_ref[...]) * SCALE
        query_ids = row_ref[0, :, slot * span : (slot + 1) * span]
        scores = jnp.where(key_ids <= query_ids, scores, -1e30)
        highest = jnp.max(scores, axis=0, keepdims=True)
        weights = jnp.exp(scores - highest)
        total = jnp.sum(weights, axis=0, keepdims=True)
        probs = (weights * (1.0 / total)).astype(BF16)
        o_ref[slot, 0] = mm(values_t, probs).T.astype(BF16)
        lt_ref[0, 0, :, slot * span : (slot + 1) * span] = highest + jnp.log(total)


def backward_kernel(parts, *refs):
    q_slots = joined_slots(refs[:parts])
    k_slots = joined_slots(refs[parts : 2 * parts])
    v_slots = joined_slots(refs[2 * parts : 3 * parts])
    do_slots = joined_slots(refs[3 * parts : -7])
    o_ref, col_ref, row_ref, lt_ref, out_ref, ka_ref, va_ref = refs[-7:]
    span = q_slots[0].shape[0]
    heads = pl.num_programs(1)
    head = pl.program_id(1)
    keys = jnp.concatenate([r[...] for r in k_slots], axis=0)
    keys_t = keys.T
    values = jnp.concatenate([r[...] for r in v_slots], axis=0)
    key_ids = col_ref[0]

    def columns(kind):
        return pl.ds(pl.multiple_of((kind * heads + head) * HEAD_DIM, HEAD_DIM), HEAD_DIM)

    for slot, q_ref in enumerate(q_slots):
        queries = q_ref[...]
        grad_out = do_slots[slot][...]
        scores = mm_nt(keys, queries) * SCALE
        query_ids = row_ref[0, :, slot * span : (slot + 1) * span]
        log_total = lt_ref[0, 0, :, slot * span : (slot + 1) * span]
        probs = jnp.exp(jnp.where(key_ids <= query_ids, scores, -1e30) - log_total)
        inner = grad_out.astype(F32) * o_ref[slot, 0].astype(F32)
        inner = jnp.sum(inner.T, axis=0, keepdims=True)
        grad_scores = (probs * (mm_nt(values, grad_out) - inner)).astype(BF16)
        out_ref[slot, 0, :, columns(0)] = (mm(keys_t, grad_scores) * SCALE).T.astype(BF16)
        key_part = mm(grad_scores, queries)
        value_part = mm(probs.astype(BF16), grad_out)
        if slot == 0:
            ka_ref[...] = key_part
            va_ref[...] = value_part
        else:
            ka_ref[...] += key_part
            va_ref[...] += value_part
    for slot in range(len(q_slots)):
        rows = slice(slot * span, (slot + 1) * span)
        out_ref[slot, 0, :, columns(1)] = (ka_ref[rows] * SCALE).astype(BF16)
        out_ref[slot, 0, :, columns(2)] = va_ref[rows].astype(BF16)


def head_spec(array, offset):
    slots, _, span, _ = array.shape
    return pl.BlockSpec((slots, 1, span, HEAD_DIM), lambda s, h: (0, s, 0, offset + h))


def table_specs(length):
    return (
        pl.BlockSpec((1, length, 1), lambda s, h: (s, 0, 0)),
        pl.BlockSpec((1, 1, length), lambda s, h: (s, 0, 0)),
        pl.BlockSpec((1, 1, 1, length), lambda s, h: (s, h, 0, 0)),
    )


def attend_forward(joined, ids_col, ids_row):
    slots = sum(part.shape[0] for part in joined)
    _, seqs, span, width = joined[0].shape
    heads = width // (3 * HEAD_DIM)
    col, row, total = table_specs(slots * span)
    out = jax.ShapeDtypeStruct((slots, seqs, span, heads * HEAD_DIM), BF16)
    return pl.pallas_call(
        functools.partial(forward_kernel, len(joined)),
        grid=(seqs, heads),
        in_specs=[head_spec(part, kind * heads) for kind in range(3) for part in joined] + [col, row],
        out_specs=[head_spec(out, 0), total],
        out_shape=[out, jax.ShapeDtypeStruct((seqs, heads, 1, slots * span), F32)],
        name="attend_forward",
    )(*(tuple(joined) * 3), ids_col, ids_row)


def attend_backward(joined, attended, grad_attended, ids_col, ids_row, log_total):
    slots = sum(part.shape[0] for part in joined)
    _, seqs, span, width = joined[0].shape
    heads = width // (3 * HEAD_DIM)
    col, row, total = table_specs(slots * span)
    return pl.pallas_call(
        functools.partial(backward_kernel, len(joined)),
        grid=(seqs, heads),
        in_specs=[head_spec(part, kind * heads) for kind in range(3) for part in joined]
        + [head_spec(part, 0) for part in grad_attended]
        + [head_spec(attended, 0), col, row, total],
        out_specs=pl.BlockSpec((slots, 1, span, width), lambda s, h: (0, s, 0, 0)),
        out_shape=jax.ShapeDtypeStruct((slots, seqs, span, width), BF16),
        scratch_shapes=[pltpu.VMEM((slots * span, HEAD_DIM), F32)] * 2,
        name="attend_backward",
    )(*(tuple(joined) * 3), *grad_attended, attended, ids_col, ids_row, log_total)


def after(value, *others):
    return lax.optimization_barrier((value,) + others)[0]


def shards(
    n,
    m,
    layer_input,
    block_ids,
    out_grad,
    qkv_weight,
    out_weight,
    up_weight,
    down_weight,
    attn_gain,
    attn_shift,
    query_bias,
    value_bias,
    out_bias,
    mlp_gain,
    mlp_shift,
    up_bias,
    down_bias,
):
    seqs, span, width = layer_input.shape
    rows = seqs * span
    pos = lax.axis_index("ctx")
    cols = qkv_weight.shape[2]
    hidden_cols = up_weight.shape[1]

    def move(value, shift):
        return lax.ppermute(value, "ctx", [(i, (i + shift) % n) for i in range(n)])

    last = []

    def hop(value, shift, *guards):
        out = move(after(value, *last, *guards), shift)
        last[:] = [out]
        return out

    def exchange(slots, sign):
        slots = list(lax.optimization_barrier(tuple(slots) + tuple(last)))[: len(slots)]
        out = [slots[0]] + [move(slots[s], sign * s) for s in range(1, n)]
        last[:] = out[1:]
        return out

    def plus(left, right):
        return left.astype(F32) + right.astype(F32)

    pieces = (
        attn_gain,
        attn_shift,
        query_bias,
        value_bias,
        out_bias,
        mlp_gain,
        mlp_shift,
        down_bias,
        up_bias,
    )
    packed = jnp.concatenate(pieces)
    packed_size = packed.shape[0]
    out_chunks = [out_weight.T]
    out_chunks.append(hop(out_chunks[0], -1))
    everyone = lax.all_to_all(jnp.broadcast_to(packed, (n, packed_size)), "ctx", 0, 0, tiled=True)
    out_chunks.append(hop(out_chunks[1], -1, everyone))
    everyone = lax.all_to_all(
        jnp.broadcast_to(everyone.reshape(1, n * packed_size), (m, n * packed_size)), "dp", 0, 0, tiled=True
    )
    for _ in range(3, n):
        out_chunks.append(hop(out_chunks[-1], -1, everyone))
    everyone = everyone.reshape(m * n, packed_size).astype(F32)
    full = []
    offset = 0
    for piece in pieces:
        size = piece.shape[0]
        full.append(everyone[:, offset : offset + size].reshape(1, m * n * size))
        offset += size
    gain_one, shift_one, bias_query, bias_value, bias_out, gain_two, shift_two, bias_down, bias_up = full
    bias_query = lax.dynamic_slice_in_dim(bias_query, pos * cols, cols, 1)
    bias_value = lax.dynamic_slice_in_dim(bias_value, pos * cols, cols, 1)
    bias_up = lax.dynamic_slice_in_dim(bias_up, pos * hidden_cols, hidden_cols, 1)
    joined_bias = jnp.concatenate([bias_query, jnp.zeros_like(bias_query), bias_value], axis=1)

    qkv_full = lax.all_gather(qkv_weight.reshape(-1, 3 * cols), "dp", axis=0, tiled=True)
    out_t = lax.all_gather(jnp.concatenate(out_chunks, axis=1), "dp", axis=0, tiled=True)
    up_full = lax.all_gather(up_weight, "dp", axis=0, tiled=True)
    down_t = lax.all_gather(down_weight.T, "dp", axis=0, tiled=True)

    x_slots = [layer_input.reshape(rows, width)]
    for _ in range(1, n):
        x_slots.append(hop(x_slots[-1], 1))

    order = (pos - jnp.arange(n)) % n
    ids = jnp.take(block_ids.reshape(seqs, n, span), order, axis=1).reshape(seqs, n * span)
    ids_col = ids[:, :, None]
    ids_row = ids[:, None, :]

    resid = x_slots[0].astype(F32)
    _, unit_one, inv_one = normalize(resid, gain_one, shift_one)
    act_parts = [
        normalize(jnp.concatenate(part, axis=0).astype(F32), gain_one, shift_one)[0].astype(BF16)
        for part in (x_slots[:-1], x_slots[-1:])
    ]
    joined = [
        (mm(part, qkv_full) + joined_bias).astype(BF16).reshape(-1, seqs, span, 3 * cols) for part in act_parts
    ]
    grad_low = out_grad.reshape(rows, width)
    dy_slots = [grad_low, hop(grad_low, 1, joined[0])]
    attended, log_total = attend_forward(joined, ids_col, ids_row)
    attended_rows = jnp.concatenate(exchange([a.reshape(rows, cols) for a in attended], -1), axis=1)
    dy_slots.append(hop(dy_slots[-1], 1))
    after_attn = resid + mm_nt(attended_rows, out_t) + bias_out
    normed_two, unit_two, inv_two = normalize(after_attn, gain_two, shift_two)

    def feed_forward(act, dy):
        pre_act = mm(act, up_full) + bias_up
        phi = 0.5 * (1.0 + lax.erf(pre_act * (1.0 / math.sqrt(2.0))))
        hidden = (pre_act * phi).astype(BF16)
        slope = phi + pre_act * (jnp.exp(-0.5 * pre_act * pre_act) * (1.0 / math.sqrt(2.0 * math.pi)))
        grad_pre = (mm(dy, down_t) * slope).astype(BF16)
        return hidden, grad_pre, mm_nt(grad_pre, up_full).astype(BF16)

    acts = [normed_two.astype(BF16)]
    acts.append(hop(acts[0], 1))
    results = [feed_forward(acts[0], dy_slots[0])]
    for s in range(2, n):
        acts.append(hop(acts[-1], 1, results[-1][2]))
        results.append(feed_forward(acts[s - 1], dy_slots[s - 1]))
        if s < n - 1:
            dy_slots.append(hop(dy_slots[-1], 1, results[-1][2] if s > 2 else acts[-1]))
    lows = [mm_nt(r[0], down_t).astype(BF16) for r in results]
    total = hop(results[1][2], 1, results[-1][2], *lows)
    results.append(feed_forward(acts[-1], dy_slots[-1]))
    lows.append(mm_nt(results[-1][0], down_t).astype(BF16))
    hidden, grad_pre, parts_two = zip(*results)
    act_two = jnp.concatenate(acts, axis=0)
    grad_pre_all = jnp.concatenate(grad_pre, axis=0)
    grad_up = mm_tn(act_two, grad_pre_all).astype(BF16)
    up_part = lax.psum_scatter(grad_up, "dp", scatter_dimension=0, tiled=True).astype(F32)
    grad_down_t = mm_tn(jnp.concatenate(dy_slots, axis=0), jnp.concatenate(hidden, axis=0)).astype(BF16)
    down_part = lax.psum_scatter(grad_down_t, "dp", scatter_dimension=0, tiled=True).astype(F32).T
    grad_up_bias = jnp.sum(grad_pre_all, axis=0, dtype=F32)
    for s in range(2, n):
        total = hop(plus(total, parts_two[s]).astype(BF16), 1, results[-1][2] if s < n - 1 else grad_up)
    low_total = hop(lows[1], 1, grad_down_t)

    grad_act_two = plus(total, parts_two[0])
    grad_from_two, grad_gain_two, grad_shift_two = normalize_back(grad_act_two, gain_two, unit_two, inv_two)
    grad_top = grad_low.astype(F32)
    grad_after = grad_top + grad_from_two
    grad_branch = grad_after.astype(BF16)
    grad_attended_rows = mm(grad_branch, out_t).astype(BF16)
    grad_attended = exchange([grad_attended_rows[:, s * cols : (s + 1) * cols] for s in range(n)], 1)
    grad_attended = [r.reshape(1, seqs, span, cols) for r in grad_attended]
    grad_out_t = mm_tn(grad_branch, attended_rows).astype(BF16)
    out_part = lax.psum_scatter(grad_out_t, "dp", scatter_dimension=0, tiled=True)
    for s in range(2, n - 1):
        low_total = hop(plus(low_total, lows[s]).astype(BF16), 1, grad_out_t)
    grad_joined = attend_backward(joined, attended, grad_attended, ids_col, ids_row, log_total)
    grad_joined = grad_joined.reshape(n, rows, 3 * cols)
    parts_one = [mm_nt(grad_joined[s], qkv_full).astype(BF16) for s in range(n)]
    total = hop(parts_one[1], 1)
    grad_qkv = mm_tn(jnp.concatenate(act_parts, axis=0), grad_joined.reshape(n * rows, 3 * cols)).astype(BF16)
    qkv_part = lax.psum_scatter(grad_qkv, "dp", scatter_dimension=0, tiled=True).astype(F32)
    qkv_part = qkv_part.reshape(qkv_weight.shape)
    for s in range(2, n):
        total = hop(plus(total, parts_one[s]).astype(BF16), 1, grad_qkv, parts_one[0])
    grad_act_one = plus(total, parts_one[0])
    low_total = plus(hop(plus(low_total, lows[n - 1]).astype(BF16), 1), lows[0])
    layer_output = after_attn + low_total + bias_down
    out_sum = out_part[:, cols : 2 * cols]
    for s in list(range(2, n)) + [0]:
        out_sum = plus(hop(out_sum.astype(BF16), -1), out_part[:, s * cols : (s + 1) * cols])
    out_part = out_sum.T
    grad_joined = grad_joined.reshape(n * rows, 3 * cols)

    grad_from_one, _, _ = normalize_back(grad_act_one, gain_one, unit_one, inv_one)
    input_grad = grad_after + grad_from_one
    grad_gain_one = 0.0
    grad_shift_one = 0.0
    for part, x in zip(parts_one, x_slots):
        part = part.astype(F32)
        grad_gain_one += jnp.sum(part * normalize(x.astype(F32), 1.0, 0.0)[1], axis=0)
        grad_shift_one += jnp.sum(part, axis=0)
    grad_out_bias = jnp.sum(grad_branch, axis=0, dtype=F32)
    grad_down_bias = jnp.sum(grad_top, axis=0)
    sums = jnp.sum(grad_joined, axis=0, dtype=F32)

    def placed(part, length):
        return lax.dynamic_update_slice_in_dim(jnp.zeros((length,), F32), part, pos * part.shape[0], 0)

    vectors = (
        grad_gain_one,
        grad_shift_one,
        placed(sums[:cols], width),
        placed(sums[2 * cols :], width),
        grad_out_bias,
        grad_gain_two,
        grad_shift_two,
        grad_down_bias,
        placed(grad_up_bias, n * hidden_cols),
    )
    table = jnp.concatenate([v.reshape(m * n, -1) for v in vectors], axis=1)
    table = lax.all_to_all(table.reshape(m, n * packed_size), "dp", 0, 0, tiled=True)
    table = jnp.sum(table, axis=0).reshape(n, packed_size)
    table = jnp.sum(lax.all_to_all(table, "ctx", 0, 0, tiled=True), axis=0)
    vector_grads = []
    offset = 0
    for piece in pieces:
        size = piece.shape[0]
        vector_grads.append(table[offset : offset + size])
        offset += size
    g = vector_grads
    return (
        layer_output.astype(BF16).reshape(seqs, span, width),
        input_grad.reshape(seqs, span, width),
        qkv_part,
        out_part,
        up_part,
        down_part,
        g[0],
        g[1],
        g[2],
        g[3],
        g[4],
        g[5],
        g[6],
        g[8],
        g[7],
    )


def solution(mesh):
    vector = P(("dp", "ctx"))
    tokens = P("dp", "ctx", None)
    weights = (P("dp", None, "ctx"), P("ctx", "dp"), P("dp", "ctx"), P("ctx", "dp"))

    def body(*args):
        return shards(mesh.shape["ctx"], mesh.shape["dp"], *args)

    return jax.shard_map(
        body,
        mesh=mesh,
        in_specs=(tokens, P("dp", None), tokens) + weights + (vector,) * 9,
        out_specs=(tokens, tokens) + weights + (vector,) * 9,
        check_vma=False,
    )
```

```python
import functools
import math

import jax
import jax.numpy as jnp
from jax import lax
from jax.experimental import pallas as pl
from jax.experimental.pallas import tpu as pltpu
from jax.sharding import PartitionSpec as P


HEAD_DIM = 128
SCALE = 1.0 / math.sqrt(HEAD_DIM)
BF16 = jnp.bfloat16
F32 = jnp.float32
LAST = (((1,), (1,)), ((), ()))
FIRST = (((0,), (0,)), ((), ()))


def mm(left, right):
    return jnp.dot(left, right, preferred_element_type=F32)


def mm_nt(left, right):
    return lax.dot_general(left, right, LAST, preferred_element_type=F32)


def normalize(values, gain, shift):
    middle = jnp.mean(values, axis=-1, keepdims=True)
    centred = values - middle
    spread = jnp.mean(centred * centred, axis=-1, keepdims=True)
    inv_std = lax.rsqrt(spread + 1e-05)
    unit_rows = centred * inv_std
    return (unit_rows * gain + shift, unit_rows, inv_std)


def normalize_back(grad_rows, gain, unit_rows, inv_std):
    scaled = grad_rows * gain
    centred = scaled - jnp.mean(scaled, axis=-1, keepdims=True)
    centred = centred - unit_rows * jnp.mean(scaled * unit_rows, axis=-1, keepdims=True)
    return (centred * inv_std, jnp.sum(grad_rows * unit_rows, axis=0), jnp.sum(grad_rows, axis=0))


def joined_slots(refs):
    return [ref.at[slot, 0] for ref in refs for slot in range(ref.shape[0])]


def forward_kernel(parts, *refs):
    q_slots = joined_slots(refs[:parts])
    k_slots = joined_slots(refs[parts : 2 * parts])
    v_slots = joined_slots(refs[2 * parts : 3 * parts])
    col_ref, row_ref, o_ref, lt_ref = refs[3 * parts :]
    span = q_slots[0].shape[0]
    keys = jnp.concatenate([r[...] for r in k_slots], axis=0)
    values_t = jnp.concatenate([r[...] for r in v_slots], axis=0).T
    key_ids = col_ref[0]
    for slot, q_ref in enumerate(q_slots):
        scores = mm_nt(keys, q_ref[...]) * SCALE
        query_ids = row_ref[0, :, slot * span : (slot + 1) * span]
        scores = jnp.where(key_ids <= query_ids, scores, -1e30)
        highest = jnp.max(scores, axis=0, keepdims=True)
        weights = jnp.exp(scores - highest)
        total = jnp.sum(weights, axis=0, keepdims=True)
        probs = (weights * (1.0 / total)).astype(BF16)
        o_ref[slot, 0] = mm(values_t, probs).T.astype(BF16)
        lt_ref[0, 0, :, slot * span : (slot + 1) * span] = highest + jnp.log(total)


def backward_kernel(parts, *refs):
    q_slots = joined_slots(refs[:parts])
    k_slots = joined_slots(refs[parts : 2 * parts])
    v_slots = joined_slots(refs[2 * parts : 3 * parts])
    *do_slots, o_ref, col_ref, row_ref, lt_ref, out_ref, ka_ref, va_ref = refs[3 * parts :]
    span = q_slots[0].shape[0]
    heads = pl.num_programs(1)
    head = pl.program_id(1)
    keys = jnp.concatenate([r[...] for r in k_slots], axis=0)
    keys_t = keys.T
    values = jnp.concatenate([r[...] for r in v_slots], axis=0)
    key_ids = col_ref[0]

    def columns(kind):
        return pl.ds(pl.multiple_of((kind * heads + head) * HEAD_DIM, HEAD_DIM), HEAD_DIM)

    for slot, q_ref in enumerate(q_slots):
        queries = q_ref[...]
        grad_out = do_slots[slot][0, 0]
        scores = mm_nt(keys, queries) * SCALE
        query_ids = row_ref[0, :, slot * span : (slot + 1) * span]
        log_total = lt_ref[0, 0, :, slot * span : (slot + 1) * span]
        probs = jnp.exp(jnp.where(key_ids <= query_ids, scores, -1e30) - log_total)
        inner = grad_out.astype(F32) * o_ref[slot, 0].astype(F32)
        inner = jnp.sum(inner.T, axis=0, keepdims=True)
        grad_scores = (probs * (mm_nt(values, grad_out) - inner)).astype(BF16)
        out_ref[slot, 0, :, columns(0)] = (mm(keys_t, grad_scores) * SCALE).T.astype(BF16)
        key_part = mm(grad_scores, queries)
        value_part = mm(probs.astype(BF16), grad_out)
        if slot == 0:
            ka_ref[...] = key_part
            va_ref[...] = value_part
        else:
            ka_ref[...] += key_part
            va_ref[...] += value_part
    for slot in range(len(q_slots)):
        rows = slice(slot * span, (slot + 1) * span)
        out_ref[slot, 0, :, columns(1)] = (ka_ref[rows] * SCALE).astype(BF16)
        out_ref[slot, 0, :, columns(2)] = va_ref[rows].astype(BF16)


def head_spec(array, offset):
    slots, _, span, _ = array.shape
    return pl.BlockSpec((slots, 1, span, HEAD_DIM), lambda s, h: (0, s, 0, offset + h))


def table_specs(length):
    return (
        pl.BlockSpec((1, length, 1), lambda s, h: (s, 0, 0)),
        pl.BlockSpec((1, 1, length), lambda s, h: (s, 0, 0)),
        pl.BlockSpec((1, 1, 1, length), lambda s, h: (s, h, 0, 0)),
    )


def attend_forward(joined, ids_col, ids_row):
    slots = sum(part.shape[0] for part in joined)
    _, seqs, span, width = joined[0].shape
    heads = width // (3 * HEAD_DIM)
    col, row, total = table_specs(slots * span)
    out = jax.ShapeDtypeStruct((slots, seqs, span, heads * HEAD_DIM), BF16)
    return pl.pallas_call(
        functools.partial(forward_kernel, len(joined)),
        grid=(seqs, heads),
        in_specs=[head_spec(part, kind * heads) for kind in range(3) for part in joined] + [col, row],
        out_specs=[head_spec(out, 0), total],
        out_shape=[out, jax.ShapeDtypeStruct((seqs, heads, 1, slots * span), F32)],
        name="af",
    )(*(tuple(joined) * 3), ids_col, ids_row)


def attend_backward(joined, attended, grad_attended, ids_col, ids_row, log_total):
    slots = sum(part.shape[0] for part in joined)
    _, seqs, span, width = joined[0].shape
    heads = width // (3 * HEAD_DIM)
    col, row, total = table_specs(slots * span)
    return pl.pallas_call(
        functools.partial(backward_kernel, len(joined)),
        grid=(seqs, heads),
        in_specs=[head_spec(part, kind * heads) for kind in range(3) for part in joined]
        + [head_spec(part, 0) for part in grad_attended]
        + [head_spec(attended, 0), col, row, total],
        out_specs=pl.BlockSpec((slots, 1, span, width), lambda s, h: (0, s, 0, 0)),
        out_shape=jax.ShapeDtypeStruct((slots, seqs, span, width), BF16),
        scratch_shapes=[pltpu.VMEM((slots * span, HEAD_DIM), F32)] * 2,
        name="ab",
    )(*(tuple(joined) * 3), *grad_attended, attended, ids_col, ids_row, log_total)


def product_kernel(count, parity_ref, *refs):
    out_ref = refs[-1]
    total = lax.dot_general(refs[0][...], refs[count][...], FIRST, preferred_element_type=F32)
    for left, right in zip(refs[1:count], refs[count + 1 : 2 * count]):
        total += lax.dot_general(left[...], right[...], FIRST, preferred_element_type=F32)
    if len(refs) > 2 * count + 1:
        total += refs[2 * count][...].astype(F32)
    out_ref[...] = total.astype(BF16)


def half_product(parity, lefts, rights, blocks, rows, add=()):
    width = lefts[0][0].shape[1] // blocks
    columns = rights[0][0].shape[1]

    def left_spec(row):
        return pl.BlockSpec((rows, width), lambda i, parity: (row, 2 * i + parity[0]))

    def right_spec(row):
        return pl.BlockSpec((rows, columns), lambda i, parity: (row, 0))

    block = pl.BlockSpec((width, columns), lambda i, parity: (i, 0))
    return pl.pallas_call(
        functools.partial(product_kernel, len(lefts)),
        grid_spec=pltpu.PrefetchScalarGridSpec(
            num_scalar_prefetch=1,
            grid=(blocks // 2,),
            in_specs=[left_spec(row) for _, row in lefts] + [right_spec(row) for _, row in rights] + [block] * len(add),
            out_specs=block,
        ),
        out_shape=jax.ShapeDtypeStruct((width * blocks // 2, columns), BF16),
        name="hp",
    )(parity, *(a for a, _ in lefts), *(a for a, _ in rights), *add)


def after(value, *others):
    return lax.optimization_barrier((value,) + others)[0]


def shards(
    n,
    m,
    layer_input,
    block_ids,
    out_grad,
    qkv_weight,
    out_weight,
    up_weight,
    down_weight,
    attn_gain,
    attn_shift,
    query_bias,
    value_bias,
    out_bias,
    mlp_gain,
    mlp_shift,
    up_bias,
    down_bias,
):
    seqs, span, width = layer_input.shape
    rows = seqs * span
    pos = lax.axis_index("ctx")
    cols = qkv_weight.shape[2]
    hidden_cols = up_weight.shape[1]

    def move(value, shift):
        return lax.ppermute(value, "ctx", [(i, (i + shift) % n) for i in range(n)])

    last = []

    def hop(value, shift, *guards):
        value = after(value, *last, *guards)
        out = move(value, shift)
        last[:] = [out]
        return out

    def exchange(slots, sign):
        slots = lax.optimization_barrier(tuple(slots) + tuple(last))[: len(slots)]
        out = [slots[0]] + [move(slots[s], sign * s) for s in range(1, n)]
        last[:] = out[1:]
        return out

    def in_order(blocks):
        return jnp.stack([lax.dynamic_index_in_dim(blocks, (c - pos) % n, 0, keepdims=False) for c in range(n)])

    core = lax.axis_index("dp") % 2
    planes = [list(range(c, m, 2)) for c in range(2)]

    def scatter_product(lefts, rights):
        theirs = half_product(jnp.reshape(1 - core, (1,)), lefts, rights, m, rows)
        given = lax.ppermute(theirs, "dp", [(i, i ^ 1) for i in range(m)])
        own = half_product(jnp.reshape(core, (1,)), lefts, rights, m, rows, (given,))
        out = lax.psum_scatter(own, "dp", scatter_dimension=0, tiled=True, axis_index_groups=planes)
        return out, own

    def plus(left, right):
        return left.astype(F32) + right.astype(F32)

    pieces = (
        attn_gain,
        attn_shift,
        query_bias,
        value_bias,
        out_bias,
        mlp_gain,
        mlp_shift,
        down_bias,
        up_bias,
    )
    packed = jnp.concatenate(pieces)
    packed_size = packed.shape[0]
    qkv_flat = qkv_weight.reshape(-1, 3 * cols)

    def riding(block, lines):
        short = -lines.shape[-1] % (16 * block.shape[-1])
        lines = jnp.pad(lines, ((0, 0),) * (lines.ndim - 1) + ((0, short),))
        return jnp.concatenate([block, lines.reshape(block.shape[:-2] + (-1, block.shape[-1]))], axis=-2)

    out_rows = out_weight.shape[0]
    carried = [riding(out_weight, packed)]
    for _ in range(1, n):
        carried.append(move(carried[-1], -1))
    x_slots = [layer_input.reshape(rows, width)]
    x_slots.append(hop(x_slots[0], 1))
    out_chunks = [c[:out_rows].T for c in carried]
    lines = [c[out_rows:].reshape(-1)[:packed_size] for c in carried]
    everyone = in_order(jnp.stack(lines))
    everyone = lax.all_to_all(
        jnp.broadcast_to(everyone.reshape(1, n * packed_size), (m, n * packed_size)), "dp", 0, 0, tiled=True
    )
    everyone = everyone.reshape(m * n, packed_size).astype(F32)
    full = []
    offset = 0
    for piece in pieces:
        size = piece.shape[0]
        full.append(everyone[:, offset : offset + size].reshape(1, m * n * size))
        offset += size
    gain_one, shift_one, bias_query, bias_value, bias_out, gain_two, shift_two, bias_down, bias_up = full
    bias_query = lax.dynamic_slice_in_dim(bias_query, pos * cols, cols, 1)
    bias_value = lax.dynamic_slice_in_dim(bias_value, pos * cols, cols, 1)
    bias_up = lax.dynamic_slice_in_dim(bias_up, pos * hidden_cols, hidden_cols, 1)
    joined_bias = jnp.concatenate([bias_query, jnp.zeros_like(bias_query), bias_value], axis=1)

    qkv_full = lax.all_gather(qkv_flat, "dp", axis=0, tiled=True)
    out_t = lax.all_gather(jnp.concatenate(list(out_chunks), axis=1), "dp", axis=0, tiled=True)
    up_full = lax.all_gather(up_weight, "dp", axis=0, tiled=True)
    down_t = lax.all_gather(down_weight.T, "dp", axis=0, tiled=True)

    for _ in range(2, n):
        x_slots.append(hop(x_slots[-1], 1))

    order = (pos - jnp.arange(n)) % n
    ids = jnp.take(block_ids.reshape(seqs, n, span), order, axis=1).reshape(seqs, n * span)
    ids_col = ids[:, :, None]
    ids_row = ids[:, None, :]

    resid = x_slots[0].astype(F32)
    _, unit_one, inv_one = normalize(resid, gain_one, shift_one)
    act_parts = [
        normalize(jnp.concatenate(part, axis=0).astype(F32), gain_one, shift_one)[0].astype(BF16)
        for part in (x_slots[:-1], x_slots[-1:])
    ]
    joined = []
    for part in act_parts:
        joined.append((mm(part, qkv_full) + joined_bias).astype(BF16).reshape(-1, seqs, span, 3 * cols))
    grad_low = out_grad.reshape(rows, width)
    dy_slots = [grad_low, hop(grad_low, 1)]
    attended, log_total = attend_forward(joined, ids_col, ids_row)
    attended_rows = jnp.concatenate(exchange([a.reshape(rows, cols) for a in attended], -1), axis=1)
    dy_slots.append(hop(dy_slots[-1], 1))
    after_attn = resid + mm_nt(attended_rows, out_t) + bias_out
    normed_two, unit_two, inv_two = normalize(after_attn, gain_two, shift_two)

    def lift(s):
        pre_act = mm(acts[s], up_full) + bias_up
        phi = 0.5 * (1.0 + lax.erf(pre_act * (1.0 / math.sqrt(2.0))))
        hidden = (pre_act * phi).astype(BF16)
        slope = phi + pre_act * (jnp.exp(-0.5 * pre_act * pre_act) * (1.0 / math.sqrt(2.0 * math.pi)))
        return hidden, slope

    def lift_back(s):
        grad_pre = (mm(after(dy_slots[s], gates[s]), down_t) * lifted[s][1]).astype(BF16)
        return grad_pre, lax.optimization_barrier(mm_nt(grad_pre, up_full).astype(BF16))

    acts = [normed_two.astype(BF16)]
    acts.append(hop(acts[0], 1))
    for s in range(2, n):
        acts.append(hop(acts[-1], 1))
        if s < n - 1:
            dy_slots.append(hop(dy_slots[-1], 1))
    lifted = [lift(s) for s in range(n)]
    gates = [acts[min(2, n - 1)], dy_slots[-1]] + acts[-1:] * (n - 2)
    backs = [lift_back(s) for s in range(n)]
    hidden = [h for h, _ in lifted]
    grad_pre, parts_two = zip(*backs)
    grad_up_bias = sum(jnp.sum(g, axis=0, dtype=F32) for g in grad_pre)

    def chunks(arrays):
        return [(a, 0) for a in arrays]

    total = hop(parts_two[1], 1)
    for s in range(2, n):
        total = hop(plus(total, parts_two[s]).astype(BF16), 1)
    up_part, _ = scatter_product(chunks(acts), chunks(grad_pre))
    down_part, _ = scatter_product(chunks(dy_slots), chunks(hidden))
    up_part = up_part.astype(F32)
    down_part = down_part.astype(F32).T
    lows = []
    for s in range(n):
        lows.append(lax.optimization_barrier(mm_nt(hidden[s], down_t).astype(BF16)))
    low_total = hop(lows[1], 1)

    grad_act_two = plus(total, parts_two[0])
    grad_from_two, grad_gain_two, grad_shift_two = normalize_back(grad_act_two, gain_two, unit_two, inv_two)
    grad_top = grad_low.astype(F32)
    grad_after = grad_top + grad_from_two
    grad_branch = grad_after.astype(BF16)
    grad_attended_rows = mm(grad_branch, out_t).astype(BF16)
    grad_attended = exchange(jnp.split(grad_attended_rows, n, axis=1), 1)
    grad_attended = [g.reshape(1, seqs, span, cols) for g in grad_attended]
    out_part, _ = scatter_product([(grad_branch, 0)], [(attended_rows, 0)])
    for s in range(2, n - 1):
        low_total = hop(plus(low_total, lows[s]).astype(BF16), 1)
    grad_joined = attend_backward(joined, attended, grad_attended, ids_col, ids_row, log_total)
    grad_joined = grad_joined.reshape(n, rows, 3 * cols)
    parts_one = []
    for s in range(n):
        parts_one.append(lax.optimization_barrier(mm_nt(grad_joined[s], qkv_full).astype(BF16)))
    total = hop(parts_one[1], 1)
    act_chunks = [(part, k) for part in act_parts for k in range(part.shape[0] // rows)]
    grad_joined = grad_joined.reshape(n * rows, 3 * cols)
    qkv_part, _ = scatter_product(act_chunks, [(grad_joined, k) for k in range(n)])
    qkv_part = qkv_part.astype(F32).reshape(qkv_weight.shape)
    total = hop(plus(total, parts_one[2]).astype(BF16), 1)
    grad_gain_one = 0.0
    grad_shift_one = 0.0
    for part, x in zip(lax.optimization_barrier((*parts_one, total))[:n], x_slots):
        part = part.astype(F32)
        grad_gain_one += jnp.sum(part * normalize(x.astype(F32), 1.0, 0.0)[1], axis=0)
        grad_shift_one += jnp.sum(part, axis=0)
    grad_out_bias = jnp.sum(grad_branch, axis=0, dtype=F32)
    grad_down_bias = jnp.sum(grad_top, axis=0)
    sums = jnp.sum(grad_joined, axis=0, dtype=F32)

    def placed(part, length):
        return lax.dynamic_update_slice_in_dim(jnp.zeros((length,), F32), part, pos * part.shape[0], 0)

    vectors = (
        grad_gain_one,
        grad_shift_one,
        placed(sums[:cols], width),
        placed(sums[2 * cols :], width),
        grad_out_bias,
        grad_gain_two,
        grad_shift_two,
        grad_down_bias,
        placed(grad_up_bias, n * hidden_cols),
    )
    table = after(jnp.concatenate([v.reshape(m * n, -1) for v in vectors], axis=1), lows[0])
    table = lax.all_to_all(table.reshape(m, n * packed_size), "dp", 0, 0, tiled=True)
    table = jnp.sum(table, axis=0).reshape(n, packed_size)
    for s in range(3, n):
        total = hop(plus(total, parts_one[s]).astype(BF16), 1)
    grad_act_one = plus(total, parts_one[0])
    low_total = plus(hop(plus(low_total, lows[n - 1]).astype(BF16), 1), lows[0])
    rows_out = out_part.shape[0]
    high = table.astype(BF16)
    halves = jnp.concatenate([high, (table - high.astype(F32)).astype(BF16)], axis=1)
    slots = [
        riding(part, lax.dynamic_index_in_dim(halves, (pos + s) % n, 0, keepdims=False))
        for s, part in enumerate(jnp.split(out_part, n, axis=1))
    ]
    swapped = sum(slot.astype(F32) for slot in exchange(slots, 1))
    table = swapped[rows_out:].reshape(-1)[: 2 * packed_size]
    out_part = swapped[:rows_out]
    layer_output = after_attn + low_total + bias_down
    table = table[:packed_size] + table[packed_size:]
    out_part = out_part.T

    grad_from_one, _, _ = normalize_back(grad_act_one, gain_one, unit_one, inv_one)
    input_grad = grad_after + grad_from_one
    vector_grads = []
    offset = 0
    for piece in pieces:
        size = piece.shape[0]
        vector_grads.append(table[offset : offset + size])
        offset += size
    g = vector_grads
    return (
        layer_output.astype(BF16).reshape(seqs, span, width),
        input_grad.reshape(seqs, span, width),
        qkv_part,
        out_part,
        up_part,
        down_part,
        g[0],
        g[1],
        g[2],
        g[3],
        g[4],
        g[5],
        g[6],
        g[8],
        g[7],
    )


def solution(mesh):
    vector = P(("dp", "ctx"))
    tokens = P("dp", "ctx", None)
    weights = (P("dp", None, "ctx"), P("ctx", "dp"), P("dp", "ctx"), P("ctx", "dp"))

    def body(*args):
        return shards(mesh.shape["ctx"], mesh.shape["dp"], *args)

    return jax.shard_map(
        body,
        mesh=mesh,
        in_specs=(tokens, P("dp", None), tokens) + weights + (vector,) * 9,
        out_specs=(tokens, tokens) + weights + (vector,) * 9,
        check_vma=False,
    )
```
